32 devices in a mesh: rows: 4 (over x, core), cols: 8 (over z, y).
Axes of the slice: x: 2, y: 2, z: 4, core: 2. Of those that a mesh axis runs over, the one named last changes fastest.
Arguments:
- image: bfloat16 [48, 64, 2048], P(None, 'rows', 'cols'), may hold values from -6 to 6
- perturb: float32 [48, 64, 2048], P(None, 'rows', 'cols'), may hold values from -0.5 to 0.5
- target: bfloat16 [48, 32, 1024], P(None, 'rows', 'cols'), may hold values from -6 to 6
- kernel_one: float32 [48, 48, 3, 3], replicated, may hold values from -0.3125 to 0.3125
- kernel_two: float32 [48, 48, 3, 3], replicated, may hold values from -0.3125 to 0.3125
- moment_one: float32 [48, 48, 3, 3], replicated, may hold values from -6 to 6
- moment_two: float32 [48, 48, 3, 3], replicated, may hold values from -6 to 6
Outputs:
- new_perturb: float32 [48, 64, 2048], P(None, 'rows', 'cols')
- prediction: bfloat16 [48, 32, 1024], P(None, 'rows', 'cols')
- new_kernel_one: float32 [48, 48, 3, 3], replicated
- new_kernel_two: float32 [48, 48, 3, 3], replicated
- new_moment_one: float32 [48, 48, 3, 3], replicated
- new_moment_two: float32 [48, 48, 3, 3], replicated
The draws below stay inside these ranges and needn't reach their ends.
All inputs are finite; a program needn't handle non-finite values.
Results may differ from the reference program's by a relative error of at most 0.0085.
Values may be sent and summed in bfloat16 or wider, within the bound.
A program may use at most 128 MiB of HBM per device.

```python
import jax
import jax.numpy as jnp
from jax import lax

C = 48
REPLAYS = 3
HEIGHT = 64
WIDTH = 2048


def steps_of(key, shape, cuts, smallest, largest):
    def one(dim, parts):
        heights = jax.random.uniform(jax.random.fold_in(jax.random.fold_in(key, 6), dim), (parts,), jnp.float32, smallest / len(cuts), largest / len(cuts))
        return jnp.repeat(jnp.exp(heights), shape[dim] // parts).reshape((-1,) + (1,) * (len(shape) - dim - 1))

    factor_of = one(*cuts[0])
    for cut in cuts[1:]:
        factor_of = factor_of * one(*cut)
    return factor_of


def normal_values(key, shape, width, most, cuts=(), dtype=jnp.bfloat16):
    result = width * jax.random.normal(key, shape, jnp.float32)
    if cuts:
        result = result * steps_of(key, shape, cuts, -0.22, 0.18)
    return jnp.clip(result, -most, most).astype(dtype)


def setup_inputs(seed: int = 0) -> dict:
    seeds = jax.random.split(jax.random.key(seed), 8)
    return {
        "image": normal_values(seeds[0], (C, HEIGHT, WIDTH), 1.0, 6.0, ((1, 4), (2, 8))),
        "perturb": jnp.clip(jax.random.uniform(seeds[1], (C, HEIGHT, WIDTH), jnp.float32, -0.5, 0.5) * steps_of(seeds[1], (C, HEIGHT, WIDTH), ((1, 4), (2, 8)), -0.4, 0.0), -0.5, 0.5),
        "target": normal_values(seeds[2], (C, HEIGHT // 2, WIDTH // 2), 1.0, 6.0, ((1, 4), (2, 8))),
        "kernel_one": normal_values(seeds[3], (C, C, 3, 3), (9 * C) ** -0.5, 0.3125, (), jnp.float32),
        "kernel_two": normal_values(seeds[4], (C, C, 3, 3), (9 * C) ** -0.5, 0.3125, (), jnp.float32),
        "moment_one": normal_values(seeds[5], (C, C, 3, 3), 1.0, 6.0, (), jnp.float32),
        "moment_two": normal_values(seeds[6], (C, C, 3, 3), 1.0, 6.0, (), jnp.float32),
    }


step_size = 0.5
clip_bound = 0.5
momentum_rate = 0.9
learn_rate = 0.005
mean_epsilon = 1e-06
numbers = ('NCHW', 'OIHW', 'NCHW')

def rounded(values):
    return lax.optimization_barrier(values.astype(jnp.bfloat16)).astype(jnp.float32)

def dilated_conv(source, kernel):
    return lax.conv_general_dilated(source[None], kernel, (1, 1), ((2, 2), (2, 2)), rhs_dilation=(2, 2), dimension_numbers=numbers, precision=lax.Precision.HIGHEST)[0]

def strided_conv(source, kernel):
    return lax.conv_general_dilated(source[None], kernel, (2, 2), ((1, 1), (1, 1)), dimension_numbers=numbers, precision=lax.Precision.HIGHEST)[0]

def silu_slope(pre_value):
    sigmoid_value = jax.nn.sigmoid(pre_value)
    return sigmoid_value * (1.0 + pre_value * (1.0 - sigmoid_value))

def normed_update(kernel, moment, gradient):
    moment = momentum_rate * moment + gradient / jnp.sqrt(jnp.mean(gradient * gradient) + mean_epsilon)
    return (kernel - learn_rate * moment, moment)

def reference(image, perturb, target, kernel_one, kernel_two, moment_one, moment_two):
    target_wide = target.astype(jnp.float32)
    predict = jnp.zeros(target.shape, jnp.float32)
    for replay in range(REPLAYS):
        fast_one = rounded(kernel_one)
        fast_two = rounded(kernel_two)
        attacked = rounded(image.astype(jnp.float32) + perturb)
        hidden_pre, pull_one = jax.vjp(dilated_conv, attacked, fast_one)
        hidden = rounded(jax.nn.silu(hidden_pre))
        predict, pull_two = jax.vjp(strided_conv, hidden, fast_two)
        residual = rounded(predict - target_wide)
        hidden_grad, grad_two = pull_two(residual)
        pre_grad = rounded(hidden_grad * silu_slope(hidden_pre))
        input_grad, grad_one = pull_one(pre_grad)
        perturb = jnp.clip(perturb + step_size * jnp.tanh(input_grad), -clip_bound, clip_bound)
        kernel_one, moment_one = normed_update(kernel_one, moment_one, grad_one)
        kernel_two, moment_two = normed_update(kernel_two, moment_two, grad_two)
    return (perturb, predict.astype(jnp.bfloat16), kernel_one, kernel_two, moment_one, moment_two)
```

```python
import functools

import jax
import jax.numpy as jnp
import ml_dtypes
import numpy as np
from jax import lax
from jax.experimental import pallas as pl
from jax.experimental.pallas import tpu as pltpu
from jax.sharding import PartitionSpec as P

REPLAYS = 3

step_size = 0.5
clip_bound = 0.5
momentum_rate = 0.9
learn_rate = 0.005
mean_epsilon = 1e-06

MESH = pl.DeviceIdType.MESH
BF16 = jnp.bfloat16
F32 = jnp.float32
RIM = 3
LANES = 128
SECOND = 64
VMEM_LIMIT = 56 * 1024 * 1024
WHOLE = pl.BlockSpec(memory_space=pltpu.VMEM)


class Flat:
    def __init__(self, channels, rows, cols):
        self.channels, self.rows, self.cols = channels, rows, cols
        self.pitch = cols + 16
        self.total = -(-((rows + 2 * RIM) * self.pitch) // LANES) * LANES
        self.lift = rows * self.pitch
        self.edge = -(-(RIM * self.pitch) // LANES) * LANES
        first = RIM * self.pitch
        self.own_low = first // LANES * LANES
        self.own_high = -(-(first + self.lift) // LANES) * LANES
        self.down_from = self.own_low
        self.band = self.total - (self.down_from + self.lift)
        assert self.lift % LANES == 0 and self.edge <= self.band

    def at(self, row, col):
        return (row + RIM) * self.pitch + col + RIM

    def places(self):
        groups = []
        lane = 0
        for down, right in ((0, -1), (0, 1), (-1, -1), (-1, 1), (1, -1), (1, 1)):
            rows = {0: range(self.rows), -1: range(self.rows - RIM, self.rows), 1: range(RIM)}[down]
            cols = {-1: range(self.cols - RIM, self.cols), 1: range(RIM)}[right]
            pairs = [(r, c) for r in rows for c in cols]
            groups.append(((down, right), lane, pairs))
            lane += len(pairs)
        assert lane <= LANES
        return groups

    def tables(self):
        pack = np.zeros((self.total, LANES), ml_dtypes.bfloat16)
        unpack = np.zeros((LANES, self.total), ml_dtypes.bfloat16)
        for (down, right), lane, pairs in self.places():
            for k, (r, c) in enumerate(pairs):
                pack[self.at(r, c), lane + k] = 1
                unpack[lane + k, self.at(r + down * self.rows, c + right * self.cols)] = 1
        spots = np.arange(self.total)
        where = np.zeros((8, self.total), np.int32)
        where[0] = spots // self.pitch - RIM
        where[1] = spots % self.pitch - RIM
        return pack, unpack, where


def position(axis, distance):
    count = lax.axis_size(axis)
    return lax.rem(lax.axis_index(axis) + (distance + count), count)


def beside_of(down, right):
    return {"rows": position("rows", down), "cols": position("cols", right)}


STEPS = ((0, -1), (0, 1), (-1, -1), (-1, 1), (1, -1), (1, 1))


def exchange_kernel(flat, row_count, col_count, with_sum, with_rim, *refs):
    refs = list(refs)
    if with_rim:
        own, packed = refs.pop(0), refs.pop(0)
    if with_sum:
        grad = refs.pop(0)
    if with_rim:
        above, below, beside = refs.pop(0), refs.pop(0), refs.pop(0)
    if with_sum:
        summed, part_rows, part_cols, half = refs[:4]
        refs = refs[4:]
    sends, recvs = refs

    me_row, me_col = lax.axis_index("rows"), lax.axis_index("cols")
    barrier = pltpu.get_barrier_semaphore()
    greeted = 0
    if with_sum:
        for d in range(1, row_count):
            pl.semaphore_signal(barrier, inc=1, device_id=beside_of(d, 0), device_id_type=MESH)
            greeted += 1
        for d in range(1, col_count):
            pl.semaphore_signal(barrier, inc=1, device_id=beside_of(0, d), device_id_type=MESH)
            greeted += 1
    if with_rim:
        also = [s for s in STEPS if not with_sum or 0 not in s]
        if not with_sum:
            also += [(-1, 0), (1, 0)]
        for down, right in also:
            pl.semaphore_signal(barrier, inc=1, device_id=beside_of(down, right), device_id_type=MESH)
            greeted += 1
    pl.semaphore_wait(barrier, greeted)

    used = [0]

    def send(source, target, device):
        k = used[0]
        used[0] += 1
        copy = pltpu.make_async_remote_copy(
            src_ref=source,
            dst_ref=target,
            send_sem=sends.at[k],
            recv_sem=recvs.at[k],
            device_id=device,
            device_id_type=MESH,
        )
        copy.start()
        return copy

    rim_copies = []
    first_copies = []
    if with_sum:
        tall = grad.shape[0] // row_count
        short = tall // col_count
        for d in range(1, row_count):
            there = position("rows", d)
            first_copies.append(
                send(grad.at[pl.ds(there * tall, tall)], part_rows.at[d - 1], beside_of(d, 0))
            )
    if with_rim:
        low, high = flat.lift, flat.lift + flat.edge
        rim_copies.append(send(own.at[:, :, low:high], above, beside_of(1, 0)))
        low, high = flat.down_from, flat.down_from + flat.band
        rim_copies.append(send(own.at[:, :, low:high], below, beside_of(-1, 0)))
        for k, (down, right) in enumerate(STEPS):
            rim_copies.append(send(packed, beside.at[k], beside_of(-down, -right)))
    if with_sum:
        for copy in first_copies:
            copy.wait()
        total = grad[pl.ds(me_row * tall, tall)]
        for d in range(1, row_count):
            total = total + part_rows[d - 1]
        half[...] = total
        second_copies = []
        for d in range(1, col_count):
            there = position("cols", d)
            second_copies.append(
                send(half.at[pl.ds(there * short, short)], part_cols.at[d - 1], beside_of(0, d))
            )
        for copy in second_copies:
            copy.wait()
        total = half[pl.ds(me_col * short, short)]
        for d in range(1, col_count):
            total = total + part_cols[d - 1]
        mine = pl.ds(me_row * tall + me_col * short, short)
        summed[mine] = total
        third_copies = []
        for d in range(1, col_count):
            third_copies.append(send(summed.at[mine], summed.at[mine], beside_of(0, d)))
        for copy in third_copies:
            copy.wait()
        band = pl.ds(me_row * tall, tall)
        last_copies = []
        for d in range(1, row_count):
            last_copies.append(send(summed.at[band], summed.at[band], beside_of(d, 0)))
        for copy in last_copies:
            copy.wait()
    for copy in rim_copies:
        copy.wait()


def exchange(flat, call_id, own=None, packed=None, grad=None):
    row_count, col_count = lax.axis_size("rows"), lax.axis_size("cols")
    operands, shapes, scratch = [], [], []
    count = 0
    if own is not None:
        operands += [own, packed]
        planes = own.shape[0]
        shapes += [
            jax.ShapeDtypeStruct((planes, flat.channels, flat.edge), BF16),
            jax.ShapeDtypeStruct((planes, flat.channels, flat.band), BF16),
            jax.ShapeDtypeStruct((len(STEPS),) + packed.shape, BF16),
        ]
        count += 8
    if grad is not None:
        operands.append(grad)
        shapes.append(jax.ShapeDtypeStruct(grad.shape, F32))
        tall = grad.shape[0] // row_count
        short = tall // col_count
        scratch += [
            pltpu.VMEM((row_count - 1, tall, LANES), F32),
            pltpu.VMEM((col_count - 1, short, LANES), F32),
            pltpu.VMEM((tall, LANES), F32),
        ]
        count += 2 * (row_count - 1) + 2 * (col_count - 1)
    return pl.pallas_call(
        functools.partial(
            exchange_kernel, flat, row_count, col_count, grad is not None, own is not None
        ),
        out_shape=shapes,
        in_specs=[WHOLE] * len(operands),
        out_specs=[WHOLE] * len(shapes),
        scratch_shapes=scratch + [pltpu.SemaphoreType.DMA((count,)), pltpu.SemaphoreType.DMA((count,))],
        compiler_params=pltpu.CompilerParams(
            collective_id=call_id, has_side_effects=True, vmem_limit_bytes=VMEM_LIMIT
        ),
    )(*operands)


def dot(a, b):
    return jnp.dot(a, b, preferred_element_type=F32)


def dot_nt(a, b):
    return lax.dot_general(a, b, (((1,), (1,)), ((), ())), preferred_element_type=F32)


def updated(state, moment, grad, entries):
    lane = lax.broadcasted_iota(jnp.int32, (1, LANES), 1)
    squared = jnp.sum(grad * grad, axis=0, keepdims=True)
    one = jnp.sum(jnp.where(lane < SECOND, squared, 0.0), axis=1, keepdims=True) / entries
    two = jnp.sum(jnp.where(lane >= SECOND, squared, 0.0), axis=1, keepdims=True) / entries
    scale = jnp.sqrt(jnp.where(lane < SECOND, one, two) + mean_epsilon)
    moment = momentum_rate * moment + grad / scale
    return state - learn_rate * moment, moment


def rolled(values, shift):
    if shift == 0:
        return values
    return pltpu.roll(values, (-shift) % values.shape[1], axis=1)


def merged_rim(flat, own, above, below, beside, unpack, index):
    return own


def step_kernel(flat, row_count, col_count, first, *refs):
    refs = list(refs)
    own, above, below, beside, image, perturb, state, moment = refs[:8]
    refs = refs[8:]
    if first:
        pack, unpack, where = refs[:3]
        refs = refs[3:]
        new_perturb, new_own, new_packed, new_grad, predict_out, target_out = refs[:6]
        refs = refs[6:]
    else:
        grad, target_in, pack, unpack, where = refs[:5]
        refs = refs[5:]
        new_perturb, new_own, new_packed, new_grad, predict_out, new_state, new_moment = refs[:7]
        refs = refs[7:]
    ext, attacked_cols, slope, hidden, hidden_cols, rest_cols, pre_cols, pre, wide, back, spread_weight = refs
    C, N, T = flat.channels, flat.total, flat.pitch
    taps = [(a, b) for a in range(3) for b in range(3)]
    K = 9 * C
    low, high = flat.own_low, flat.own_high

    me_row, me_col = lax.axis_index("rows"), lax.axis_index("cols")
    row, col = where[0:1, :], where[1:2, :]
    owned = ((row >= 0) & (row < flat.rows) & (col >= 0) & (col < flat.cols)).astype(F32)
    far_row, far_col = row + me_row * flat.rows, col + me_col * flat.cols
    inside = (
        (far_row >= 0)
        & (far_row < flat.rows * row_count)
        & (far_col >= 0)
        & (far_col < flat.cols * col_count)
    ).astype(F32)

    if first:
        now = state[...]
    else:
        now, later = updated(state[...], moment[...], grad[0:K, :], K * C)
        new_state[...] = now
        new_moment[...] = later
    fast = now.astype(BF16)
    eye = (
        lax.broadcasted_iota(jnp.int32, (LANES, LANES), 0)
        == lax.broadcasted_iota(jnp.int32, (LANES, LANES), 1)
    ).astype(F32).astype(BF16)
    ahead = dot_nt(eye, fast).astype(BF16)
    ahead_one, ahead_two = ahead[0:C, :], ahead[SECOND : SECOND + C, :]
    from_lane = lax.broadcasted_iota(jnp.int32, (LANES, K), 0)
    to_lane = lax.broadcasted_iota(jnp.int32, (LANES, K), 1)
    back_one = jnp.zeros((C, K), F32)
    for k in range(9):
        put = ((to_lane == from_lane + k * C) & (from_lane < C)).astype(F32).astype(BF16)
        back_one = back_one + dot(fast[k * C : (k + 1) * C, :], put)
    back_one = back_one.astype(BF16)
    four = 4 * C
    from_lane = lax.broadcasted_iota(jnp.int32, (LANES, four), 0)
    to_lane = lax.broadcasted_iota(jnp.int32, (LANES, four), 1)
    for py in range(2):
        for px in range(2):
            block = jnp.zeros((C, four), F32)
            for a, dy in ([(1, 0)] if py == 0 else [(0, 1), (2, 0)]):
                for b, dx in ([(1, 0)] if px == 0 else [(0, 1), (2, 0)]):
                    k = 3 * a + b
                    slot = 2 * dy + dx
                    put = (
                        (to_lane == from_lane - SECOND + slot * C)
                        & (from_lane >= SECOND)
                        & (from_lane < SECOND + C)
                    ).astype(F32).astype(BF16)
                    block = block + dot(fast[k * C : (k + 1) * C, :], put)
            spread_weight[(2 * py + px) * C : (2 * py + px + 1) * C, :] = block.astype(BF16)

    planes = own.shape[0]
    lane = lax.broadcasted_iota(jnp.int32, (1, LANES), 1)
    gathered = jnp.zeros((planes * C, LANES), F32)
    for k, ((down, right), start, pairs) in enumerate(flat.places()):
        there_row, there_col = me_row + down, me_col + right
        exists = (
            (there_row >= 0) & (there_row < row_count) & (there_col >= 0) & (there_col < col_count)
        )
        keep = (lane >= start) & (lane < start + len(pairs)) & exists
        gathered = gathered + jnp.where(keep, beside[k].astype(F32), 0.0)
    gathered = gathered.astype(BF16)
    has_above = jnp.where(me_row > 0, 1.0, 0.0).astype(F32)
    has_below = jnp.where(me_row < row_count - 1, 1.0, 0.0).astype(F32)
    end = flat.down_from + flat.lift
    for p in range(planes):
        ext[...] = own[p].astype(F32) + dot(gathered[p * C : (p + 1) * C, :], unpack[...])
        ext[:, 0 : flat.edge] += above[p].astype(F32) * has_above
        ext[:, end:N] += below[p].astype(F32) * has_below
        if p == 4:
            target_out[...] = ext[...].astype(BF16)
            continue
        full = ext[...]
        for k, (a, b) in enumerate(taps):
            moved = rolled(full, (a - 1) * T + (b - 1))
            attacked_cols[p, k * C : (k + 1) * C, :] = moved.astype(BF16)
        pre_value = dot(ahead_one, attacked_cols[p])
        sigmoid_value = jax.nn.sigmoid(pre_value)
        hidden[p] = pre_value * sigmoid_value * inside
        slope[p] = sigmoid_value * (1.0 + pre_value * (1.0 - sigmoid_value)) * inside
    target = (target_out if first else target_in)[...].astype(F32)

    for k, (a, b) in enumerate(taps):
        py, dy = [(1, -1), (0, 0), (1, 0)][a]
        px, dx = [(1, -1), (0, 0), (1, 0)][b]
        hidden_cols[k * C : (k + 1) * C, :] = rolled(hidden[2 * py + px], dy * T + dx).astype(BF16)
    predict = dot(ahead_two, hidden_cols[...])
    predict_out[...] = predict.astype(BF16)
    residual = (predict - target) * inside
    wide[...] = jnp.zeros(wide.shape, BF16)
    wide[SECOND : SECOND + C, :] = (residual * owned)[:, low:high].astype(BF16)
    total = dot_nt(hidden_cols[:, low:high], wide[...])
    wide[...] = jnp.zeros(wide.shape, BF16)
    for k, shift in enumerate((0, 1, T, T + 1)):
        rest_cols[k * C : (k + 1) * C, :] = rolled(residual, shift).astype(BF16)
    hidden_grad = dot(spread_weight[...], rest_cols[...])
    new_own[...] = jnp.zeros(new_own.shape, BF16)
    new_perturb[...] = jnp.zeros(new_perturb.shape, F32)
    for p in range(4):
        pre_grad = hidden_grad[p * C : (p + 1) * C, :] * slope[p]
        wide[0:C, :] = (pre_grad * owned)[:, low:high].astype(BF16)
        total = total + dot_nt(attacked_cols[p, :, low:high], wide[...])
        for k, (a, b) in enumerate(taps):
            moved = rolled(pre_grad, -((a - 1) * T + (b - 1)))
            pre_cols[k * C : (k + 1) * C, :] = moved[:, low:high].astype(BF16)
        input_grad = dot(back_one, pre_cols[...])
        moved = jnp.clip(
            perturb[p, :, low:high] + step_size * jnp.tanh(input_grad), -clip_bound, clip_bound
        )
        moved = moved * owned[:, low:high]
        new_perturb[p, :, low:high] = moved
        attacked = (image[p, :, low:high].astype(F32) + moved).astype(BF16)
        new_own[p, :, low:high] = attacked
        new_packed[p * C : (p + 1) * C, :] = dot(attacked, pack[low:high, :]).astype(BF16)
    new_grad[...] = jnp.zeros(new_grad.shape, F32)
    new_grad[0:K, :] = total


def step(flat, tables, own, rim, image, perturb, state, moment, grad, target, tall):
    first = grad is None
    C, N = flat.channels, flat.total
    K = 9 * C
    operands = [own, *rim, image, perturb, state, moment]
    if not first:
        operands += [grad, target]
    operands += list(tables)
    shapes = [
        jax.ShapeDtypeStruct((4, C, N), F32),
        jax.ShapeDtypeStruct((4, C, N), BF16),
        jax.ShapeDtypeStruct((4 * C, LANES), BF16),
        jax.ShapeDtypeStruct((tall, LANES), F32),
        jax.ShapeDtypeStruct((C, N), BF16),
    ]
    if first:
        shapes.append(jax.ShapeDtypeStruct((C, N), BF16))
    else:
        shapes += [jax.ShapeDtypeStruct((K, LANES), F32)] * 2
    width = flat.own_high - flat.own_low
    scratch = [
        pltpu.VMEM((C, N), F32),
        pltpu.VMEM((4, K, N), BF16),
        pltpu.VMEM((4, C, N), F32),
        pltpu.VMEM((4, C, N), F32),
        pltpu.VMEM((K, N), BF16),
        pltpu.VMEM((4 * C, N), BF16),
        pltpu.VMEM((K, width), BF16),
        pltpu.VMEM((C, N), F32),
        pltpu.VMEM((LANES, width), BF16),
        pltpu.VMEM((C, K), BF16),
        pltpu.VMEM((4 * C, 4 * C), BF16),
    ]
    return pl.pallas_call(
        functools.partial(step_kernel, flat, lax.axis_size("rows"), lax.axis_size("cols"), first),
        out_shape=shapes,
        in_specs=[WHOLE] * len(operands),
        out_specs=[WHOLE] * len(shapes),
        scratch_shapes=scratch,
        compiler_params=pltpu.CompilerParams(vmem_limit_bytes=VMEM_LIMIT),
    )(*operands)


def last_kernel(entries, state, moment, grad, new_state, new_moment):
    now, later = updated(state[...], moment[...], grad[0 : state.shape[0], :], entries)
    new_state[...] = now
    new_moment[...] = later


def parted(flat, block):
    C, h, w = flat.channels, flat.rows, flat.cols
    order = np.zeros((2 * w, 2 * w), np.float32)
    for c in range(w):
        order[2 * c, c] = 1
        order[2 * c + 1, w + c] = 1
    order = jnp.asarray(order, block.dtype)
    sorted_cols = jnp.dot(
        block.reshape(C * 2 * h, 2 * w),
        order,
        precision=lax.Precision.HIGHEST if block.dtype == F32 else None,
        preferred_element_type=block.dtype,
    )
    planes = sorted_cols.reshape(C, h, 2, 2, w).transpose(2, 3, 0, 1, 4).reshape(4, C, h, w)
    return laid(flat, planes)


def laid(flat, planes):
    count = planes.shape[0]
    right = flat.pitch - flat.cols - RIM
    planes = jnp.pad(planes, ((0, 0), (0, 0), (RIM, RIM), (RIM, right)))
    planes = planes.reshape(count, flat.channels, -1)
    return jnp.pad(planes, ((0, 0), (0, 0), (0, flat.total - planes.shape[2])))


def unlaid(flat, planes):
    count = planes.shape[0]
    planes = planes[:, :, : (flat.rows + 2 * RIM) * flat.pitch]
    planes = planes.reshape(count, flat.channels, flat.rows + 2 * RIM, flat.pitch)
    return planes[:, :, RIM : RIM + flat.rows, RIM : RIM + flat.cols]


def joined(flat, planes):
    C, h, w = flat.channels, flat.rows, flat.cols
    order = np.zeros((2 * w, 2 * w), np.float32)
    for c in range(w):
        order[c, 2 * c] = 1
        order[w + c, 2 * c + 1] = 1
    blocks = unlaid(flat, planes).reshape(2, 2, C, h, w).transpose(2, 3, 0, 1, 4)
    blocks = jnp.dot(
        blocks.reshape(C * 2 * h, 2 * w), jnp.asarray(order), precision=lax.Precision.HIGHEST
    )
    return blocks.reshape(C, 2 * h, 2 * w)


def stacked(one, two):
    C = one.shape[0]
    one, two = (k.transpose(2, 3, 1, 0).reshape(9 * C, C) for k in (one, two))
    one = jnp.pad(one, ((0, 0), (0, SECOND - C)))
    two = jnp.pad(two, ((0, 0), (0, SECOND - C)))
    return jnp.concatenate([one, two], axis=1)


def unstacked(both, C):
    return tuple(
        both[:, low : low + C].reshape(3, 3, C, C).transpose(3, 2, 0, 1) for low in (0, SECOND)
    )


def body(image, perturb, target, kernel_one, kernel_two, moment_one, moment_two):
    C = image.shape[0]
    flat = Flat(C, target.shape[1], target.shape[2])
    tables = tuple(jnp.asarray(t) for t in flat.tables())
    devices = lax.axis_size("rows") * lax.axis_size("cols")
    tall = -(-9 * C // (8 * devices)) * 8 * devices
    image = parted(flat, image)
    perturb = parted(flat, perturb)
    state = stacked(kernel_one, kernel_two)
    moment = stacked(moment_one, moment_two)
    own = (image.astype(F32) + perturb).astype(BF16)
    own = jnp.concatenate([own, laid(flat, target[None])], axis=0)
    packed = jnp.dot(
        own.reshape(5 * C, flat.total), tables[0], preferred_element_type=F32
    ).astype(BF16)
    rim = exchange(flat, 0, own, packed)
    grad = None
    held_target = None
    for replay in range(REPLAYS):
        results = step(
            flat, tables, own, rim, image, perturb, state, moment, grad, held_target, tall
        )
        perturb, own, packed, grad, predict = results[:5]
        if replay == 0:
            held_target = results[5]
        else:
            state, moment = results[5:]
        if replay < REPLAYS - 1:
            *rim, grad = exchange(flat, 1, own, packed, grad)
        else:
            (grad,) = exchange(flat, 2, grad=grad)
    state, moment = pl.pallas_call(
        functools.partial(last_kernel, 9 * C * C),
        out_shape=[jax.ShapeDtypeStruct(state.shape, F32)] * 2,
        in_specs=[WHOLE] * 3,
        out_specs=[WHOLE] * 2,
    )(state, moment, grad)
    new_one, new_two = unstacked(state, C)
    new_moment_one, new_moment_two = unstacked(moment, C)
    prediction = unlaid(flat, predict[None])[0]
    return (joined(flat, perturb), prediction, new_one, new_two, new_moment_one, new_moment_two)


def solution(mesh):
    in_specs = (
        P(None, "rows", "cols"),
        P(None, "rows", "cols"),
        P(None, "rows", "cols"),
        P(),
        P(),
        P(),
        P(),
    )
    out_specs = (P(None, "rows", "cols"), P(None, "rows", "cols"), P(), P(), P(), P())
    return jax.shard_map(body, mesh=mesh, in_specs=in_specs, out_specs=out_specs, check_vma=False)
```

```python
import functools

import jax
import jax.numpy as jnp
import ml_dtypes
import numpy as np
from jax import lax
from jax.experimental import pallas as pl
from jax.experimental.pallas import tpu as pltpu
from jax.sharding import PartitionSpec as P

REPLAYS = 3

step_size = 0.5
clip_bound = 0.5
momentum_rate = 0.9
learn_rate = 0.005
mean_epsilon = 1e-06

MESH = pl.DeviceIdType.MESH
BF16 = jnp.bfloat16
F32 = jnp.float32
RIM = 3
LANES = 128
SECOND = 64
VMEM_LIMIT = 56 * 1024 * 1024
WHOLE = pl.BlockSpec(memory_space=pltpu.VMEM)


class Flat:
    def __init__(self, channels, rows, cols):
        self.channels, self.rows, self.cols = channels, rows, cols
        self.pitch = cols + 16
        self.total = -(-((rows + 2 * RIM) * self.pitch) // LANES) * LANES
        self.lift = rows * self.pitch
        self.edge = -(-(RIM * self.pitch) // LANES) * LANES
        first = RIM * self.pitch
        self.own_low = first // LANES * LANES
        self.own_high = -(-(first + self.lift) // LANES) * LANES
        self.down_from = self.own_low
        self.band = self.total - (self.down_from + self.lift)
        assert self.lift % LANES == 0 and self.edge <= self.band

    def at(self, row, col):
        return (row + RIM) * self.pitch + col + RIM

    def places(self):
        groups = []
        lane = 0
        for down, right in ((0, -1), (0, 1), (-1, -1), (-1, 1), (1, -1), (1, 1)):
            rows = {0: range(self.rows), -1: range(self.rows - RIM, self.rows), 1: range(RIM)}[down]
            cols = {-1: range(self.cols - RIM, self.cols), 1: range(RIM)}[right]
            pairs = [(r, c) for r in rows for c in cols]
            groups.append(((down, right), lane, pairs))
            lane += len(pairs)
        assert lane <= LANES
        return groups

    def tables(self):
        pack = np.zeros((self.total, LANES), ml_dtypes.bfloat16)
        unpack = np.zeros((LANES, self.total), ml_dtypes.bfloat16)
        for (down, right), lane, pairs in self.places():
            for k, (r, c) in enumerate(pairs):
                pack[self.at(r, c), lane + k] = 1
                unpack[lane + k, self.at(r + down * self.rows, c + right * self.cols)] = 1
        spots = np.arange(self.total)
        where = np.zeros((8, self.total), np.int32)
        where[0] = spots // self.pitch - RIM
        where[1] = spots % self.pitch - RIM
        return pack, unpack, where


def position(axis, distance):
    count = lax.axis_size(axis)
    return lax.rem(lax.axis_index(axis) + (distance + count), count)


STEPS = ((0, -1), (0, 1), (-1, -1), (-1, 1), (1, -1), (1, 1))


def dot(a, b):
    return jnp.dot(a, b, preferred_element_type=F32)


def dot_nt(a, b):
    return lax.dot_general(a, b, (((1,), (1,)), ((), ())), preferred_element_type=F32)


def updated(state, moment, grad, entries):
    lane = lax.broadcasted_iota(jnp.int32, (1, LANES), 1)
    squared = jnp.sum(grad * grad, axis=0, keepdims=True)
    one = jnp.sum(jnp.where(lane < SECOND, squared, 0.0), axis=1, keepdims=True) / entries
    two = jnp.sum(jnp.where(lane >= SECOND, squared, 0.0), axis=1, keepdims=True) / entries
    scale = jnp.sqrt(jnp.where(lane < SECOND, one, two) + mean_epsilon)
    moment = momentum_rate * moment + grad / scale
    return state - learn_rate * moment, moment


def rolled(values, shift):
    if shift == 0:
        return values
    return pltpu.roll(values, (-shift) % values.shape[1], axis=1)


def whole_kernel(flat, row_count, col_count, *refs):
    (first_own, first_packed, image, perturb_in, state, moment, pack, unpack, where) = refs[:9]
    (perturb, predict_out, new_state, new_moment) = refs[9:13]
    (
        ext, attacked_cols, slope, hidden, hidden_cols, rest_cols, pre_cols, wide, spread_weight,
        own, packed, target, above, below, beside, target_above, target_below,
        grad, sent, part_rows, half, part_cols, summed,
        rim_sends, rim_recvs, sum_sends, sum_recvs,
    ) = refs[13:]
    C, N, T = flat.channels, flat.total, flat.pitch
    taps = [(a, b) for a in range(3) for b in range(3)]
    K = 9 * C
    low, high = flat.own_low, flat.own_high
    tall = grad.shape[0] // row_count
    levels = [1 << s for s in range(col_count.bit_length() - 1)]
    me_row, me_col = lax.axis_index("rows"), lax.axis_index("cols")

    def exists(down, right):
        return (
            (me_row + down >= 0)
            & (me_row + down < row_count)
            & (me_col + right >= 0)
            & (me_col + right < col_count)
        )

    def partner(level):
        return me_col + level - 2 * level * lax.rem(me_col // level, 2)

    def signal(device):
        pl.semaphore_signal(barrier, inc=1, device_id=device, device_id_type=MESH)

    barrier = pltpu.get_barrier_semaphore()
    greeted = row_count - 1 + len(levels)
    for d in range(1, row_count):
        signal({"rows": position("rows", d), "cols": me_col})
    for level in levels:
        signal({"rows": me_row, "cols": partner(level)})
    for down, right in STEPS:
        there = exists(down, right)
        pl.when(there)(
            functools.partial(signal, {"rows": me_row + down, "cols": me_col + right})
        )
        greeted = greeted + there.astype(jnp.int32)
    pl.semaphore_wait(barrier, greeted)

    def copy_of(source, target, sends, recvs, device):
        return pltpu.make_async_remote_copy(
            src_ref=source,
            dst_ref=target,
            send_sem=sends,
            recv_sem=recvs,
            device_id=device,
            device_id_type=MESH,
        )

    def rim_copies(from_own, from_packed, to_above, to_below, to_beside, k):
        copies = []

        def add(source, target, down, right):
            i = len(copies)
            device = {"rows": me_row + down, "cols": me_col + right}
            copy = copy_of(source, target, rim_sends.at[k, i], rim_recvs.at[k, i], device)
            copies.append((copy, exists(down, right), exists(-down, -right)))

        one, two = flat.lift, flat.lift + flat.edge
        add(from_own.at[:, :, one:two], to_above, 1, 0)
        one, two = flat.down_from, flat.down_from + flat.band
        add(from_own.at[:, :, one:two], to_below, -1, 0)
        if from_packed is not None:
            for j, (down, right) in enumerate(STEPS):
                add(from_packed, to_beside.at[j], -down, -right)
        return copies

    def start(copies):
        for copy, there, _ in copies:
            pl.when(there)(copy.start)

    def finish(copies):
        for copy, there, here in copies:
            pl.when(there)(copy.wait_send)
            pl.when(here)(copy.wait_recv)

    def rim_of(k):
        return rim_copies(own.at[k], packed.at[k], above.at[k], below.at[k], beside.at[k], k)

    own[0] = first_own[0:4]
    packed[0] = first_packed[...]
    begin = rim_of(0)
    start(begin)
    extra = rim_copies(first_own.at[4:5], None, target_above, target_below, None, REPLAYS + 1)
    start(extra)

    row, col = where[0:1, :], where[1:2, :]
    owned = ((row >= 0) & (row < flat.rows) & (col >= 0) & (col < flat.cols)).astype(F32)
    far_row, far_col = row + me_row * flat.rows, col + me_col * flat.cols
    inside = (
        (far_row >= 0)
        & (far_row < flat.rows * row_count)
        & (far_col >= 0)
        & (far_col < flat.cols * col_count)
    ).astype(F32)
    perturb[...] = perturb_in[...]
    new_state[...] = state[...]
    new_moment[...] = moment[...]
    wide[...] = jnp.zeros(wide.shape, BF16)
    own[1:] = jnp.zeros((REPLAYS,) + own.shape[1:], BF16)
    packed[1:] = jnp.zeros((REPLAYS,) + packed.shape[1:], BF16)
    grad[...] = jnp.zeros(grad.shape, F32)
    lane = lax.broadcasted_iota(jnp.int32, (1, LANES), 1)
    has_above, has_below = me_row > 0, me_row < row_count - 1
    end = flat.down_from + flat.lift
    eye = (
        lax.broadcasted_iota(jnp.int32, (LANES, LANES), 0)
        == lax.broadcasted_iota(jnp.int32, (LANES, LANES), 1)
    ).astype(F32).astype(BF16)

    def chosen(packs, height):
        gathered = jnp.zeros((height, LANES), F32)
        for j, ((down, right), from_lane, pairs) in enumerate(flat.places()):
            keep = (lane >= from_lane) & (lane < from_lane + len(pairs)) & exists(down, right)
            gathered = gathered + jnp.where(keep, packs(j).astype(F32), 0.0)
        return gathered.astype(BF16)

    def extend(block, gathered, top, bottom):
        ext[...] = block.astype(F32) + dot(gathered, unpack[...])
        ext[:, 0 : flat.edge] += jnp.where(has_above, top.astype(F32), 0.0)
        ext[:, end:N] += jnp.where(has_below, bottom.astype(F32), 0.0)

    finish(begin)
    finish(extra)
    gathered = chosen(lambda j: beside[0, j, 4 * C : 5 * C], C)
    extend(first_own[4], gathered, target_above[0], target_below[0])
    target[...] = ext[...]

    def sum_copies(k):
        rows_out = []
        for d in range(1, row_count):
            there = position("rows", d)
            rows_out.append(
                copy_of(
                    sent.at[k, pl.ds(there * tall, tall)],
                    part_rows.at[k, d - 1],
                    sum_sends.at[k, d - 1],
                    sum_recvs.at[k, d - 1],
                    {"rows": there, "cols": me_col},
                )
            )
        cols_out = []
        for i, level in enumerate(levels):
            at = row_count - 1 + i
            cols_out.append(
                copy_of(
                    half.at[k, i],
                    part_cols.at[k, i],
                    sum_sends.at[k, at],
                    sum_recvs.at[k, at],
                    {"rows": me_row, "cols": partner(level)},
                )
            )
        band = pl.ds(me_row * tall, tall)
        back_out = []
        for d in range(1, row_count):
            at = row_count - 2 + len(levels) + d
            back_out.append(
                copy_of(
                    summed.at[k, band],
                    summed.at[k, band],
                    sum_sends.at[k, at],
                    sum_recvs.at[k, at],
                    {"rows": position("rows", d), "cols": me_col},
                )
            )
        return rows_out, cols_out, back_out

    def replay(k):
        fast = new_state[...].astype(BF16)
        ahead = dot_nt(eye, fast).astype(BF16)
        ahead_one, ahead_two = ahead[0:C, :], ahead[SECOND : SECOND + C, :]
        from_lane = lax.broadcasted_iota(jnp.int32, (LANES, K), 0)
        to_lane = lax.broadcasted_iota(jnp.int32, (LANES, K), 1)
        back_one = jnp.zeros((C, K), F32)
        for i in range(9):
            put = ((to_lane == from_lane + i * C) & (from_lane < C)).astype(F32).astype(BF16)
            back_one = back_one + dot(fast[i * C : (i + 1) * C, :], put)
        back_one = back_one.astype(BF16)
        four = 4 * C
        from_lane = lax.broadcasted_iota(jnp.int32, (LANES, four), 0)
        to_lane = lax.broadcasted_iota(jnp.int32, (LANES, four), 1)
        for py in range(2):
            for px in range(2):
                block = jnp.zeros((C, four), F32)
                for a, dy in ([(1, 0)] if py == 0 else [(0, 1), (2, 0)]):
                    for b, dx in ([(1, 0)] if px == 0 else [(0, 1), (2, 0)]):
                        i = 3 * a + b
                        slot = 2 * dy + dx
                        put = (
                            (to_lane == from_lane - SECOND + slot * C)
                            & (from_lane >= SECOND)
                            & (from_lane < SECOND + C)
                        ).astype(F32).astype(BF16)
                        block = block + dot(fast[i * C : (i + 1) * C, :], put)
                spread_weight[(2 * py + px) * C : (2 * py + px + 1) * C, :] = block.astype(BF16)

        gathered = chosen(lambda j: beside[k, j, 0 : 4 * C], 4 * C)
        for p in range(4):
            extend(own[k, p], gathered[p * C : (p + 1) * C, :], above[k, p], below[k, p])
            full = ext[...]
            for i, (a, b) in enumerate(taps):
                moved = rolled(full, (a - 1) * T + (b - 1))
                attacked_cols[p, i * C : (i + 1) * C, :] = moved.astype(BF16)
            pre_value = dot(ahead_one, attacked_cols[p])
            sigmoid_value = jax.nn.sigmoid(pre_value)
            hidden[p] = pre_value * sigmoid_value * inside
            slope[p] = sigmoid_value * (1.0 + pre_value * (1.0 - sigmoid_value)) * inside
        for i, (a, b) in enumerate(taps):
            py, dy = [(1, -1), (0, 0), (1, 0)][a]
            px, dx = [(1, -1), (0, 0), (1, 0)][b]
            moved = rolled(hidden[2 * py + px], dy * T + dx)
            hidden_cols[i * C : (i + 1) * C, :] = moved.astype(BF16)
        predict = dot(ahead_two, hidden_cols[...])
        predict_out[...] = predict.astype(BF16)
        residual = (predict - target[...]) * inside
        wide[0:C, :] = jnp.zeros((C, high - low), BF16)
        wide[SECOND : SECOND + C, :] = (residual * owned)[:, low:high].astype(BF16)
        total = dot_nt(hidden_cols[:, low:high], wide[...])
        wide[SECOND : SECOND + C, :] = jnp.zeros((C, high - low), BF16)
        for i, shift in enumerate((0, 1, T, T + 1)):
            rest_cols[i * C : (i + 1) * C, :] = rolled(residual, shift).astype(BF16)
        hidden_grad = dot(spread_weight[...], rest_cols[...])
        for p in range(4):
            pre_grad = hidden_grad[p * C : (p + 1) * C, :] * slope[p]
            hidden[p] = pre_grad
            wide[0:C, :] = (pre_grad * owned)[:, low:high].astype(BF16)
            total = total + dot_nt(attacked_cols[p, :, low:high], wide[...])
        grad[0:K, :] = total
        sent[k] = grad[...].astype(BF16)
        rows_out, cols_out, back_out = sum_copies(k)
        for copy in rows_out:
            copy.start()

        def input_side(p):
            pre_grad = hidden[p]
            for i, (a, b) in enumerate(taps):
                moved = rolled(pre_grad, -((a - 1) * T + (b - 1)))
                pre_cols[i * C : (i + 1) * C, :] = moved[:, low:high].astype(BF16)
            input_grad = dot(back_one, pre_cols[...])
            moved = jnp.clip(
                perturb[p, :, low:high] + step_size * jnp.tanh(input_grad), -clip_bound, clip_bound
            )
            moved = moved * owned[:, low:high]
            perturb[p, :, low:high] = moved
            attacked = (image[p, :, low:high].astype(F32) + moved).astype(BF16)
            own[k + 1, p, :, low:high] = attacked
            packed[k + 1, p * C : (p + 1) * C, :] = dot(attacked, pack[low:high, :]).astype(BF16)

        input_side(0)
        for copy in rows_out:
            copy.wait()
        part = grad[pl.ds(pl.multiple_of(me_row * tall, 8), tall)]
        for d in range(1, row_count):
            part = part + part_rows[k, d - 1].astype(F32)
        for i in range(len(levels)):
            half[k, i] = part.astype(BF16)
            cols_out[i].start()
            if i < 2:
                input_side(i + 1)
            if i == 1:
                input_side(3)
                following = rim_of(k + 1)
                start(following)
            cols_out[i].wait()
            part = half[k, i].astype(F32) + part_cols[k, i].astype(F32)
        summed[k, pl.ds(pl.multiple_of(me_row * tall, 16), tall)] = part.astype(BF16)
        for copy in back_out:
            copy.start()
        for copy in back_out:
            copy.wait()
        now, later = updated(
            new_state[...], new_moment[...], summed[k, 0:K, :].astype(F32), K * C
        )
        new_state[...] = now
        new_moment[...] = later
        finish(following)

    @pl.loop(0, REPLAYS)
    def _(k):
        replay(k)


def whole(flat, tables, own, packed, image, perturb, state, moment, tall):
    C, N = flat.channels, flat.total
    K = 9 * C
    row_count, col_count = lax.axis_size("rows"), lax.axis_size("cols")
    levels = col_count.bit_length() - 1
    width = flat.own_high - flat.own_low
    short = tall // row_count
    operands = [own, packed, image, perturb, state, moment, *tables]
    shapes = [
        jax.ShapeDtypeStruct((4, C, N), F32),
        jax.ShapeDtypeStruct((C, N), BF16),
        jax.ShapeDtypeStruct((K, LANES), F32),
        jax.ShapeDtypeStruct((K, LANES), F32),
    ]
    slots = REPLAYS + 1
    sums = 2 * (row_count - 1) + levels
    scratch = [
        pltpu.VMEM((C, N), F32),
        pltpu.VMEM((4, K, N), BF16),
        pltpu.VMEM((4, C, N), F32),
        pltpu.VMEM((4, C, N), F32),
        pltpu.VMEM((K, N), BF16),
        pltpu.VMEM((4 * C, N), BF16),
        pltpu.VMEM((K, width), BF16),
        pltpu.VMEM((LANES, width), BF16),
        pltpu.VMEM((4 * C, 4 * C), BF16),
        pltpu.VMEM((slots, 4, C, N), BF16),
        pltpu.VMEM((slots, 5 * C, LANES), BF16),
        pltpu.VMEM((C, N), F32),
        pltpu.VMEM((slots, 4, C, flat.edge), BF16),
        pltpu.VMEM((slots, 4, C, flat.band), BF16),
        pltpu.VMEM((slots, len(STEPS), 5 * C, LANES), BF16),
        pltpu.VMEM((1, C, flat.edge), BF16),
        pltpu.VMEM((1, C, flat.band), BF16),
        pltpu.VMEM((tall, LANES), F32),
        pltpu.VMEM((REPLAYS, tall, LANES), BF16),
        pltpu.VMEM((REPLAYS, row_count - 1, short, LANES), BF16),
        pltpu.VMEM((REPLAYS, levels, short, LANES), BF16),
        pltpu.VMEM((REPLAYS, levels, short, LANES), BF16),
        pltpu.VMEM((REPLAYS, tall, LANES), BF16),
        pltpu.SemaphoreType.DMA((slots + 1, 8)),
        pltpu.SemaphoreType.DMA((slots + 1, 8)),
        pltpu.SemaphoreType.DMA((REPLAYS, sums)),
        pltpu.SemaphoreType.DMA((REPLAYS, sums)),
    ]
    return pl.pallas_call(
        functools.partial(whole_kernel, flat, row_count, col_count),
        out_shape=shapes,
        in_specs=[WHOLE] * len(operands),
        out_specs=[WHOLE] * len(shapes),
        scratch_shapes=scratch,
        compiler_params=pltpu.CompilerParams(
            collective_id=0, has_side_effects=True, vmem_limit_bytes=VMEM_LIMIT
        ),
    )(*operands)


def parted(flat, block):
    C, h, w = flat.channels, flat.rows, flat.cols
    order = np.zeros((2 * w, 2 * w), np.float32)
    for c in range(w):
        order[2 * c, c] = 1
        order[2 * c + 1, w + c] = 1
    order = jnp.asarray(order, block.dtype)
    sorted_cols = jnp.dot(
        block.reshape(C * 2 * h, 2 * w),
        order,
        precision=lax.Precision.HIGHEST if block.dtype == F32 else None,
        preferred_element_type=block.dtype,
    )
    planes = sorted_cols.reshape(C, h, 2, 2, w).transpose(2, 3, 0, 1, 4).reshape(4, C, h, w)
    return laid(flat, planes)


def laid(flat, planes):
    count = planes.shape[0]
    right = flat.pitch - flat.cols - RIM
    planes = jnp.pad(planes, ((0, 0), (0, 0), (RIM, RIM), (RIM, right)))
    planes = planes.reshape(count, flat.channels, -1)
    return jnp.pad(planes, ((0, 0), (0, 0), (0, flat.total - planes.shape[2])))


def unlaid(flat, planes):
    count = planes.shape[0]
    planes = planes[:, :, : (flat.rows + 2 * RIM) * flat.pitch]
    planes = planes.reshape(count, flat.channels, flat.rows + 2 * RIM, flat.pitch)
    return planes[:, :, RIM : RIM + flat.rows, RIM : RIM + flat.cols]


def joined(flat, planes):
    C, h, w = flat.channels, flat.rows, flat.cols
    order = np.zeros((2 * w, 2 * w), np.float32)
    for c in range(w):
        order[c, 2 * c] = 1
        order[w + c, 2 * c + 1] = 1
    blocks = unlaid(flat, planes).reshape(2, 2, C, h, w).transpose(2, 3, 0, 1, 4)
    blocks = jnp.dot(
        blocks.reshape(C * 2 * h, 2 * w), jnp.asarray(order), precision=lax.Precision.HIGHEST
    )
    return blocks.reshape(C, 2 * h, 2 * w)


def stacked(one, two):
    C = one.shape[0]
    one, two = (k.transpose(2, 3, 1, 0).reshape(9 * C, C) for k in (one, two))
    one = jnp.pad(one, ((0, 0), (0, SECOND - C)))
    two = jnp.pad(two, ((0, 0), (0, SECOND - C)))
    return jnp.concatenate([one, two], axis=1)


def unstacked(both, C):
    return tuple(
        both[:, low : low + C].reshape(3, 3, C, C).transpose(3, 2, 0, 1) for low in (0, SECOND)
    )


def body(image, perturb, target, kernel_one, kernel_two, moment_one, moment_two):
    C = image.shape[0]
    flat = Flat(C, target.shape[1], target.shape[2])
    tables = tuple(jnp.asarray(t) for t in flat.tables())
    pieces = 16 * lax.axis_size("rows")
    tall = -(-9 * C // pieces) * pieces
    image = parted(flat, image)
    perturb = parted(flat, perturb)
    state = stacked(kernel_one, kernel_two)
    moment = stacked(moment_one, moment_two)
    own = (image.astype(F32) + perturb).astype(BF16)
    own = jnp.concatenate([own, laid(flat, target[None])], axis=0)
    packed = jnp.dot(
        own.reshape(5 * C, flat.total), tables[0], preferred_element_type=F32
    ).astype(BF16)
    perturb, predict, state, moment = whole(
        flat, tables, own, packed, image, perturb, state, moment, tall
    )
    new_one, new_two = unstacked(state, C)
    new_moment_one, new_moment_two = unstacked(moment, C)
    prediction = unlaid(flat, predict[None])[0]
    return (joined(flat, perturb), prediction, new_one, new_two, new_moment_one, new_moment_two)


def solution(mesh):
    in_specs = (
        P(None, "rows", "cols"),
        P(None, "rows", "cols"),
        P(None, "rows", "cols"),
        P(),
        P(),
        P(),
        P(),
    )
    out_specs = (P(None, "rows", "cols"), P(None, "rows", "cols"), P(), P(), P(), P())
    return jax.shard_map(body, mesh=mesh, in_specs=in_specs, out_specs=out_specs, check_vma=False)
```

```python
import functools

import jax
import jax.numpy as jnp
import ml_dtypes
import numpy as np
from jax import lax
from jax.experimental import pallas as pl
from jax.experimental.pallas import tpu as pltpu
from jax.sharding import PartitionSpec as P

REPLAYS = 3

step_size = 0.5
clip_bound = 0.5
momentum_rate = 0.9
learn_rate = 0.005
mean_epsilon = 1e-06

MESH = pl.DeviceIdType.MESH
BF16 = jnp.bfloat16
F32 = jnp.float32
RIM = 3
LANES = 128
SECOND = 64
VMEM_LIMIT = 56 * 1024 * 1024
WHOLE = pl.BlockSpec(memory_space=pltpu.VMEM)


class Flat:
    def __init__(self, channels, rows, cols):
        self.channels, self.rows, self.cols = channels, rows, cols
        self.pitch = cols + 16
        self.total = -(-((rows + 2 * RIM) * self.pitch) // LANES) * LANES
        self.lift = rows * self.pitch
        self.edge = -(-(RIM * self.pitch) // LANES) * LANES
        first = RIM * self.pitch
        self.own_low = first // LANES * LANES
        self.own_high = -(-(first + self.lift) // LANES) * LANES
        self.down_from = self.own_low
        self.band = self.total - (self.down_from + self.lift)
        assert self.lift % LANES == 0 and self.edge <= self.band

    def at(self, row, col):
        return (row + RIM) * self.pitch + col + RIM

    def places(self):
        groups = []
        lane = 0
        for down, right in ((0, -1), (0, 1), (-1, -1), (-1, 1), (1, -1), (1, 1)):
            rows = {0: range(self.rows), -1: range(self.rows - RIM, self.rows), 1: range(RIM)}[down]
            cols = {-1: range(self.cols - RIM, self.cols), 1: range(RIM)}[right]
            pairs = [(r, c) for r in rows for c in cols]
            groups.append(((down, right), lane, pairs))
            lane += len(pairs)
        assert lane <= LANES
        return groups

    def tables(self):
        pack = np.zeros((self.total, LANES), ml_dtypes.bfloat16)
        unpack = np.zeros((LANES, self.total), ml_dtypes.bfloat16)
        for (down, right), lane, pairs in self.places():
            for k, (r, c) in enumerate(pairs):
                pack[self.at(r, c), lane + k] = 1
                unpack[lane + k, self.at(r + down * self.rows, c + right * self.cols)] = 1
        spots = np.arange(self.total)
        where = np.zeros((8, self.total), np.int32)
        where[0] = spots // self.pitch - RIM
        where[1] = spots % self.pitch - RIM
        return pack, unpack, where


def position(axis, distance):
    count = lax.axis_size(axis)
    return lax.rem(lax.axis_index(axis) + (distance + count), count)


STEPS = ((0, -1), (0, 1), (-1, -1), (-1, 1), (1, -1), (1, 1))


def dot(a, b):
    return jnp.dot(a, b, preferred_element_type=F32)


def dot_nt(a, b):
    return lax.dot_general(a, b, (((1,), (1,)), ((), ())), preferred_element_type=F32)


def updated(state, moment, grad, entries):
    lane = lax.broadcasted_iota(jnp.int32, (1, LANES), 1)
    squared = jnp.sum(grad * grad, axis=0, keepdims=True)
    one = jnp.sum(jnp.where(lane < SECOND, squared, 0.0), axis=1, keepdims=True) / entries
    two = jnp.sum(jnp.where(lane >= SECOND, squared, 0.0), axis=1, keepdims=True) / entries
    scale = jnp.sqrt(jnp.where(lane < SECOND, one, two) + mean_epsilon)
    moment = momentum_rate * moment + grad / scale
    return state - learn_rate * moment, moment


def rolled(values, shift):
    if shift == 0:
        return values
    return pltpu.roll(values, (-shift) % values.shape[1], axis=1)


def whole_kernel(flat, row_count, col_count, *refs):
    (image_in, perturb_in, target_in, state, moment, pack, unpack, where) = refs[:8]
    (perturb_out, predict_out, new_state, new_moment) = refs[8:12]
    (
        ext, attacked_cols, slope, hidden, hidden_cols, rest_cols, pre_cols, wide, spread_weight,
        own, packed, target, above, below, beside, target_above, target_below,
        grad, sent, part_rows, half, part_cols, summed,
        rim_sends, rim_recvs, sum_sends, sum_recvs,
            image, perturb, target_own,
    ) = refs[12:]
    C, N, T = flat.channels, flat.total, flat.pitch
    taps = [(a, b) for a in range(3) for b in range(3)]
    K = 9 * C
    low, high = flat.own_low, flat.own_high
    tall = grad.shape[0] // row_count
    levels = [1 << s for s in range(col_count.bit_length() - 1)]
    me_row, me_col = lax.axis_index("rows"), lax.axis_index("cols")

    def exists(down, right):
        return (
            (me_row + down >= 0)
            & (me_row + down < row_count)
            & (me_col + right >= 0)
            & (me_col + right < col_count)
        )

    def partner(level):
        return me_col + level - 2 * level * lax.rem(me_col // level, 2)

    def signal(device):
        pl.semaphore_signal(barrier, inc=1, device_id=device, device_id_type=MESH)

    barrier = pltpu.get_barrier_semaphore()
    greeted = row_count - 1 + len(levels)
    for d in range(1, row_count):
        signal({"rows": position("rows", d), "cols": me_col})
    for level in levels:
        signal({"rows": me_row, "cols": partner(level)})
    for down, right in STEPS:
        there = exists(down, right)
        pl.when(there)(
            functools.partial(signal, {"rows": me_row + down, "cols": me_col + right})
        )
        greeted = greeted + there.astype(jnp.int32)

    row, col = where[0:1, :], where[1:2, :]
    owned = ((row >= 0) & (row < flat.rows) & (col >= 0) & (col < flat.cols)).astype(F32)
    w = flat.cols
    from_col = lax.broadcasted_iota(jnp.int32, (2 * w, 2 * w), 0)
    to_col = lax.broadcasted_iota(jnp.int32, (2 * w, 2 * w), 1)
    sorted_from = jnp.where(to_col < w, 2 * to_col, 2 * (to_col - w) + 1)
    order = (from_col == sorted_from).astype(F32)
    own[1:] = jnp.zeros((REPLAYS,) + own.shape[1:], BF16)
    packed[1:] = jnp.zeros((REPLAYS,) + packed.shape[1:], BF16)
    ext[...] = jnp.zeros(ext.shape, F32)
    perturb[...] = jnp.zeros(perturb.shape, F32)
    hidden[...] = jnp.zeros(hidden.shape, F32)
    for r in range(flat.rows):
        spot = flat.at(r, 0)
        ext[:, spot : spot + w] = target_in[r].astype(F32)
        for py in range(2):
            parts = dot(image_in[2 * r + py], order.astype(BF16))
            hidden[2 * py, :, spot : spot + w] = parts[:, :w]
            hidden[2 * py + 1, :, spot : spot + w] = parts[:, w:]
            parts = jnp.dot(
                perturb_in[2 * r + py],
                order,
                precision=lax.Precision.HIGHEST,
                preferred_element_type=F32,
            )
            perturb[2 * py, :, spot : spot + w] = parts[:, :w]
            perturb[2 * py + 1, :, spot : spot + w] = parts[:, w:]
    target_own[0] = ext[...].astype(BF16)
    packed[0, 4 * C : 5 * C, :] = dot(target_own[0], pack[...]).astype(BF16)
    for p in range(4):
        image[p] = hidden[p].astype(BF16)
        own[0, p] = (hidden[p] + perturb[p]).astype(BF16)
        packed[0, p * C : (p + 1) * C, :] = dot(own[0, p], pack[...]).astype(BF16)
    pl.semaphore_wait(barrier, greeted)

    def copy_of(source, target, sends, recvs, device):
        return pltpu.make_async_remote_copy(
            src_ref=source,
            dst_ref=target,
            send_sem=sends,
            recv_sem=recvs,
            device_id=device,
            device_id_type=MESH,
        )

    def rim_copies(from_own, from_packed, to_above, to_below, to_beside, k):
        copies = []

        def add(source, target, down, right):
            i = len(copies)
            device = {"rows": me_row + down, "cols": me_col + right}
            copy = copy_of(source, target, rim_sends.at[k, i], rim_recvs.at[k, i], device)
            copies.append((copy, exists(down, right), exists(-down, -right)))

        one, two = flat.lift, flat.lift + flat.edge
        add(from_own.at[:, :, one:two], to_above, 1, 0)
        one, two = flat.down_from, flat.down_from + flat.band
        add(from_own.at[:, :, one:two], to_below, -1, 0)
        if from_packed is not None:
            for j, (down, right) in enumerate(STEPS):
                add(from_packed, to_beside.at[j], -down, -right)
        return copies

    def start(copies):
        for copy, there, _ in copies:
            pl.when(there)(copy.start)

    def finish(copies):
        for copy, there, here in copies:
            pl.when(there)(copy.wait_send)
            pl.when(here)(copy.wait_recv)

    def rim_of(k):
        return rim_copies(own.at[k], packed.at[k], above.at[k], below.at[k], beside.at[k], k)

    begin = rim_of(0)
    start(begin)
    extra = rim_copies(target_own, None, target_above, target_below, None, REPLAYS + 1)
    start(extra)

    far_row, far_col = row + me_row * flat.rows, col + me_col * flat.cols
    inside = (
        (far_row >= 0)
        & (far_row < flat.rows * row_count)
        & (far_col >= 0)
        & (far_col < flat.cols * col_count)
    ).astype(F32)
    new_state[...] = state[...]
    new_moment[...] = moment[...]
    wide[...] = jnp.zeros(wide.shape, BF16)
    grad[...] = jnp.zeros(grad.shape, F32)
    lane = lax.broadcasted_iota(jnp.int32, (1, LANES), 1)
    has_above, has_below = me_row > 0, me_row < row_count - 1
    end = flat.down_from + flat.lift
    eye = (
        lax.broadcasted_iota(jnp.int32, (LANES, LANES), 0)
        == lax.broadcasted_iota(jnp.int32, (LANES, LANES), 1)
    ).astype(F32).astype(BF16)

    def chosen(packs, height):
        gathered = jnp.zeros((height, LANES), F32)
        for j, ((down, right), from_lane, pairs) in enumerate(flat.places()):
            keep = (lane >= from_lane) & (lane < from_lane + len(pairs)) & exists(down, right)
            gathered = gathered + jnp.where(keep, packs(j).astype(F32), 0.0)
        return gathered.astype(BF16)

    def extend(block, gathered, top, bottom):
        ext[...] = block.astype(F32) + dot(gathered, unpack[...])
        ext[:, 0 : flat.edge] += jnp.where(has_above, top.astype(F32), 0.0)
        ext[:, end:N] += jnp.where(has_below, bottom.astype(F32), 0.0)

    finish(begin)
    finish(extra)
    gathered = chosen(lambda j: beside[0, j, 4 * C : 5 * C], C)
    extend(target_own[0], gathered, target_above[0], target_below[0])
    target[...] = ext[...]

    def sum_copies(k):
        rows_out = []
        for d in range(1, row_count):
            there = position("rows", d)
            rows_out.append(
                copy_of(
                    sent.at[k, pl.ds(there * tall, tall)],
                    part_rows.at[k, d - 1],
                    sum_sends.at[k, d - 1],
                    sum_recvs.at[k, d - 1],
                    {"rows": there, "cols": me_col},
                )
            )
        cols_out = []
        for i, level in enumerate(levels):
            at = row_count - 1 + i
            cols_out.append(
                copy_of(
                    half.at[k, i],
                    part_cols.at[k, i],
                    sum_sends.at[k, at],
                    sum_recvs.at[k, at],
                    {"rows": me_row, "cols": partner(level)},
                )
            )
        band = pl.ds(me_row * tall, tall)
        back_out = []
        for d in range(1, row_count):
            at = row_count - 2 + len(levels) + d
            back_out.append(
                copy_of(
                    summed.at[k, band],
                    summed.at[k, band],
                    sum_sends.at[k, at],
                    sum_recvs.at[k, at],
                    {"rows": position("rows", d), "cols": me_col},
                )
            )
        return rows_out, cols_out, back_out

    def replay(k):
        fast = new_state[...].astype(BF16)
        ahead = dot_nt(eye, fast).astype(BF16)
        ahead_one, ahead_two = ahead[0:C, :], ahead[SECOND : SECOND + C, :]
        from_lane = lax.broadcasted_iota(jnp.int32, (LANES, K), 0)
        to_lane = lax.broadcasted_iota(jnp.int32, (LANES, K), 1)
        back_one = jnp.zeros((C, K), F32)
        for i in range(9):
            put = ((to_lane == from_lane + i * C) & (from_lane < C)).astype(F32).astype(BF16)
            back_one = back_one + dot(fast[i * C : (i + 1) * C, :], put)
        back_one = back_one.astype(BF16)
        four = 4 * C
        from_lane = lax.broadcasted_iota(jnp.int32, (LANES, four), 0)
        to_lane = lax.broadcasted_iota(jnp.int32, (LANES, four), 1)
        for py in range(2):
            for px in range(2):
                block = jnp.zeros((C, four), F32)
                for a, dy in ([(1, 0)] if py == 0 else [(0, 1), (2, 0)]):
                    for b, dx in ([(1, 0)] if px == 0 else [(0, 1), (2, 0)]):
                        i = 3 * a + b
                        slot = 2 * dy + dx
                        put = (
                            (to_lane == from_lane - SECOND + slot * C)
                            & (from_lane >= SECOND)
                            & (from_lane < SECOND + C)
                        ).astype(F32).astype(BF16)
                        block = block + dot(fast[i * C : (i + 1) * C, :], put)
                spread_weight[(2 * py + px) * C : (2 * py + px + 1) * C, :] = block.astype(BF16)

        gathered = chosen(lambda j: beside[k, j, 0 : 4 * C], 4 * C)
        for p in range(4):
            extend(own[k, p], gathered[p * C : (p + 1) * C, :], above[k, p], below[k, p])
            full = ext[...]
            for i, (a, b) in enumerate(taps):
                moved = rolled(full, (a - 1) * T + (b - 1))
                attacked_cols[p, i * C : (i + 1) * C, :] = moved.astype(BF16)
            pre_value = dot(ahead_one, attacked_cols[p])
            sigmoid_value = jax.nn.sigmoid(pre_value)
            hidden[p] = pre_value * sigmoid_value * inside
            slope[p] = sigmoid_value * (1.0 + pre_value * (1.0 - sigmoid_value)) * inside
        for i, (a, b) in enumerate(taps):
            py, dy = [(1, -1), (0, 0), (1, 0)][a]
            px, dx = [(1, -1), (0, 0), (1, 0)][b]
            moved = rolled(hidden[2 * py + px], dy * T + dx)
            hidden_cols[i * C : (i + 1) * C, :] = moved.astype(BF16)
        predict = dot(ahead_two, hidden_cols[...])
        ext[...] = predict
        residual = (predict - target[...]) * inside
        wide[0:C, :] = jnp.zeros((C, high - low), BF16)
        wide[SECOND : SECOND + C, :] = (residual * owned)[:, low:high].astype(BF16)
        total = dot_nt(hidden_cols[:, low:high], wide[...])
        wide[SECOND : SECOND + C, :] = jnp.zeros((C, high - low), BF16)
        for i, shift in enumerate((0, 1, T, T + 1)):
            rest_cols[i * C : (i + 1) * C, :] = rolled(residual, shift).astype(BF16)
        hidden_grad = dot(spread_weight[...], rest_cols[...])
        for p in range(4):
            pre_grad = hidden_grad[p * C : (p + 1) * C, :] * slope[p]
            hidden[p] = pre_grad
            wide[0:C, :] = (pre_grad * owned)[:, low:high].astype(BF16)
            total = total + dot_nt(attacked_cols[p, :, low:high], wide[...])
        grad[0:K, :] = total
        sent[k] = grad[...].astype(BF16)
        rows_out, cols_out, back_out = sum_copies(k)
        for copy in rows_out:
            copy.start()

        def input_side(p):
            pre_grad = hidden[p]
            for i, (a, b) in enumerate(taps):
                moved = rolled(pre_grad, -((a - 1) * T + (b - 1)))
                pre_cols[i * C : (i + 1) * C, :] = moved[:, low:high].astype(BF16)
            input_grad = dot(back_one, pre_cols[...])
            moved = jnp.clip(
                perturb[p, :, low:high] + step_size * jnp.tanh(input_grad), -clip_bound, clip_bound
            )
            moved = moved * owned[:, low:high]
            perturb[p, :, low:high] = moved
            attacked = (image[p, :, low:high].astype(F32) + moved).astype(BF16)
            own[k + 1, p, :, low:high] = attacked
            packed[k + 1, p * C : (p + 1) * C, :] = dot(attacked, pack[low:high, :]).astype(BF16)

        input_side(0)
        for copy in rows_out:
            copy.wait()
        part = grad[pl.ds(pl.multiple_of(me_row * tall, 8), tall)]
        for d in range(1, row_count):
            part = part + part_rows[k, d - 1].astype(F32)
        for i in range(len(levels)):
            half[k, i] = part.astype(BF16)
            cols_out[i].start()
            if i < 2:
                input_side(i + 1)
            if i == 1:
                input_side(3)
                following = rim_of(k + 1)
                start(following)
            cols_out[i].wait()
            part = half[k, i].astype(F32) + part_cols[k, i].astype(F32)
        summed[k, pl.ds(pl.multiple_of(me_row * tall, 16), tall)] = part.astype(BF16)
        for copy in back_out:
            copy.start()
        for copy in back_out:
            copy.wait()
        now, later = updated(
            new_state[...], new_moment[...], summed[k, 0:K, :].astype(F32), K * C
        )
        new_state[...] = now
        new_moment[...] = later
        finish(following)

    @pl.loop(0, REPLAYS)
    def _(k):
        replay(k)

    for r in range(flat.rows):
        spot = flat.at(r, 0)
        predict_out[r] = ext[:, spot : spot + w].astype(BF16)
        for py in range(2):
            parts = jnp.concatenate(
                [perturb[2 * py, :, spot : spot + w], perturb[2 * py + 1, :, spot : spot + w]], axis=1
            )
            perturb_out[2 * r + py] = lax.dot_general(
                parts,
                order,
                (((1,), (1,)), ((), ())),
                precision=lax.Precision.HIGHEST,
                preferred_element_type=F32,
            )


def whole(flat, tables, image, perturb, target, state, moment, tall):
    C, N = flat.channels, flat.total
    K = 9 * C
    row_count, col_count = lax.axis_size("rows"), lax.axis_size("cols")
    levels = col_count.bit_length() - 1
    width = flat.own_high - flat.own_low
    short = tall // row_count
    operands = [image, perturb, target, state, moment, *tables]
    shapes = [
        jax.ShapeDtypeStruct(perturb.shape, F32),
        jax.ShapeDtypeStruct(target.shape, BF16),
        jax.ShapeDtypeStruct((K, LANES), F32),
        jax.ShapeDtypeStruct((K, LANES), F32),
    ]
    slots = REPLAYS + 1
    sums = 2 * (row_count - 1) + levels
    scratch = [
        pltpu.VMEM((C, N), F32),
        pltpu.VMEM((4, K, N), BF16),
        pltpu.VMEM((4, C, N), F32),
        pltpu.VMEM((4, C, N), F32),
        pltpu.VMEM((K, N), BF16),
        pltpu.VMEM((4 * C, N), BF16),
        pltpu.VMEM((K, width), BF16),
        pltpu.VMEM((LANES, width), BF16),
        pltpu.VMEM((4 * C, 4 * C), BF16),
        pltpu.VMEM((slots, 4, C, N), BF16),
        pltpu.VMEM((slots, 5 * C, LANES), BF16),
        pltpu.VMEM((C, N), F32),
        pltpu.VMEM((slots, 4, C, flat.edge), BF16),
        pltpu.VMEM((slots, 4, C, flat.band), BF16),
        pltpu.VMEM((slots, len(STEPS), 5 * C, LANES), BF16),
        pltpu.VMEM((1, C, flat.edge), BF16),
        pltpu.VMEM((1, C, flat.band), BF16),
        pltpu.VMEM((tall, LANES), F32),
        pltpu.VMEM((REPLAYS, tall, LANES), BF16),
        pltpu.VMEM((REPLAYS, row_count - 1, short, LANES), BF16),
        pltpu.VMEM((REPLAYS, levels, short, LANES), BF16),
        pltpu.VMEM((REPLAYS, levels, short, LANES), BF16),
        pltpu.VMEM((REPLAYS, tall, LANES), BF16),
        pltpu.SemaphoreType.DMA((slots + 1, 8)),
        pltpu.SemaphoreType.DMA((slots + 1, 8)),
        pltpu.SemaphoreType.DMA((REPLAYS, sums)),
        pltpu.SemaphoreType.DMA((REPLAYS, sums)),
        pltpu.VMEM((4, C, N), BF16),
        pltpu.VMEM((4, C, N), F32),
        pltpu.VMEM((1, C, N), BF16),
    ]
    return pl.pallas_call(
        functools.partial(whole_kernel, flat, row_count, col_count),
        out_shape=shapes,
        in_specs=[WHOLE] * len(operands),
        out_specs=[WHOLE] * len(shapes),
        scratch_shapes=scratch,
        compiler_params=pltpu.CompilerParams(
            collective_id=0, has_side_effects=True, vmem_limit_bytes=VMEM_LIMIT
        ),
    )(*operands)


def stacked(one, two):
    C = one.shape[0]
    one, two = (k.transpose(2, 3, 1, 0).reshape(9 * C, C) for k in (one, two))
    one = jnp.pad(one, ((0, 0), (0, SECOND - C)))
    two = jnp.pad(two, ((0, 0), (0, SECOND - C)))
    return jnp.concatenate([one, two], axis=1)


def unstacked(both, C):
    return tuple(
        both[:, low : low + C].reshape(3, 3, C, C).transpose(3, 2, 0, 1) for low in (0, SECOND)
    )


def body(image, perturb, target, kernel_one, kernel_two, moment_one, moment_two):
    C = image.shape[0]
    flat = Flat(C, target.shape[1], target.shape[2])
    tables = tuple(jnp.asarray(t) for t in flat.tables())
    pieces = 16 * lax.axis_size("rows")
    tall = -(-9 * C // pieces) * pieces
    state = stacked(kernel_one, kernel_two)
    moment = stacked(moment_one, moment_two)
    image, perturb, target = (x.transpose(1, 0, 2) for x in (image, perturb, target))
    perturb, predict, state, moment = whole(
        flat, tables, image, perturb, target, state, moment, tall
    )
    new_one, new_two = unstacked(state, C)
    new_moment_one, new_moment_two = unstacked(moment, C)
    perturb, prediction = perturb.transpose(1, 0, 2), predict.transpose(1, 0, 2)
    return (perturb, prediction, new_one, new_two, new_moment_one, new_moment_two)


def solution(mesh):
    in_specs = (
        P(None, "rows", "cols"),
        P(None, "rows", "cols"),
        P(None, "rows", "cols"),
        P(),
        P(),
        P(),
        P(),
    )
    out_specs = (P(None, "rows", "cols"), P(None, "rows", "cols"), P(), P(), P(), P())
    return jax.shard_map(body, mesh=mesh, in_specs=in_specs, out_specs=out_specs, check_vma=False)
```

```python
import functools

import jax
import jax.numpy as jnp
import ml_dtypes
import numpy as np
from jax import lax
from jax.experimental import pallas as pl
from jax.experimental.pallas import tpu as pltpu
from jax.sharding import PartitionSpec as P

REPLAYS = 3

step_size = 0.5
clip_bound = 0.5
momentum_rate = 0.9
learn_rate = 0.005
mean_epsilon = 1e-06

MESH = pl.DeviceIdType.MESH
BF16 = jnp.bfloat16
F32 = jnp.float32
RIM = 3
LANES = 128
SECOND = 64
VMEM_LIMIT = 56 * 1024 * 1024
WHOLE = pl.BlockSpec(memory_space=pltpu.VMEM)


class Flat:
    def __init__(self, channels, rows, cols):
        self.channels, self.rows, self.cols = channels, rows, cols
        self.pitch = cols + 16
        self.total = -(-((rows + 2 * RIM) * self.pitch) // LANES) * LANES
        self.lift = rows * self.pitch
        self.edge = -(-(RIM * self.pitch) // LANES) * LANES
        first = RIM * self.pitch
        self.own_low = first // LANES * LANES
        self.own_high = -(-(first + self.lift) // LANES) * LANES
        self.down_from = self.own_low
        self.band = self.total - (self.down_from + self.lift)
        assert self.lift % LANES == 0 and self.edge <= self.band

    def at(self, row, col):
        return (row + RIM) * self.pitch + col + RIM

    def places(self):
        groups = []
        lane = 0
        for down, right in ((0, -1), (0, 1), (-1, -1), (-1, 1), (1, -1), (1, 1)):
            rows = {0: range(self.rows), -1: range(self.rows - RIM, self.rows), 1: range(RIM)}[down]
            cols = {-1: range(self.cols - RIM, self.cols), 1: range(RIM)}[right]
            pairs = [(r, c) for r in rows for c in cols]
            groups.append(((down, right), lane, pairs))
            lane += len(pairs)
        assert lane <= LANES
        return groups

    def tables(self):
        pack = np.zeros((self.total, LANES), ml_dtypes.bfloat16)
        unpack = np.zeros((LANES, self.total), ml_dtypes.bfloat16)
        for (down, right), lane, pairs in self.places():
            for k, (r, c) in enumerate(pairs):
                pack[self.at(r, c), lane + k] = 1
                unpack[lane + k, self.at(r + down * self.rows, c + right * self.cols)] = 1
        spots = np.arange(self.total)
        where = np.zeros((8, self.total), np.int32)
        where[0] = spots // self.pitch - RIM
        where[1] = spots % self.pitch - RIM
        return pack, unpack, where


def position(axis, distance):
    count = lax.axis_size(axis)
    return lax.rem(lax.axis_index(axis) + (distance + count), count)


STEPS = ((0, -1), (0, 1), (-1, -1), (-1, 1), (1, -1), (1, 1))


def dot(a, b):
    return jnp.dot(a, b, preferred_element_type=F32)


def dot_nt(a, b):
    return lax.dot_general(a, b, (((1,), (1,)), ((), ())), preferred_element_type=F32)


def updated(state, moment, grad, entries):
    lane = lax.broadcasted_iota(jnp.int32, (1, LANES), 1)
    squared = jnp.sum(grad * grad, axis=0, keepdims=True)
    one = jnp.sum(jnp.where(lane < SECOND, squared, 0.0), axis=1, keepdims=True) / entries
    two = jnp.sum(jnp.where(lane >= SECOND, squared, 0.0), axis=1, keepdims=True) / entries
    scale = jnp.sqrt(jnp.where(lane < SECOND, one, two) + mean_epsilon)
    moment = momentum_rate * moment + grad / scale
    return state - learn_rate * moment, moment


def rolled(values, shift):
    if shift == 0:
        return values
    return pltpu.roll(values, (-shift) % values.shape[1], axis=1)


def whole_kernel(flat, row_count, col_count, *refs):
    (image_in, perturb_in, target_in, state, moment, pack, unpack, where) = refs[:8]
    (perturb_out, predict_out, new_state, new_moment) = refs[8:12]
    (
        ext, attacked_cols, slope, hidden, hidden_cols, rest_cols, pre_cols, wide, spread_weight,
        own, packed, target, above, below, beside, target_above, target_below,
        grad, sent, part_rows, half, part_cols, summed,
        rim_sends, rim_recvs, sum_sends, sum_recvs,
            image, perturb, target_own,
    ) = refs[12:]
    C, N, T = flat.channels, flat.total, flat.pitch
    taps = [(a, b) for a in range(3) for b in range(3)]
    K = 9 * C
    low, high = flat.own_low, flat.own_high
    tall = grad.shape[0] // row_count
    levels = [1 << s for s in range(col_count.bit_length() - 1)]
    me_row, me_col = lax.axis_index("rows"), lax.axis_index("cols")

    def exists(down, right):
        return (
            (me_row + down >= 0)
            & (me_row + down < row_count)
            & (me_col + right >= 0)
            & (me_col + right < col_count)
        )

    def partner(level):
        return me_col + level - 2 * level * lax.rem(me_col // level, 2)

    def signal(device):
        pl.semaphore_signal(barrier, inc=1, device_id=device, device_id_type=MESH)

    barrier = pltpu.get_barrier_semaphore()
    greeted = row_count - 1 + len(levels)
    for d in range(1, row_count):
        signal({"rows": position("rows", d), "cols": me_col})
    for level in levels:
        signal({"rows": me_row, "cols": partner(level)})
    for down, right in STEPS:
        there = exists(down, right)
        pl.when(there)(
            functools.partial(signal, {"rows": me_row + down, "cols": me_col + right})
        )
        greeted = greeted + there.astype(jnp.int32)

    row, col = where[0:1, :], where[1:2, :]
    owned = ((row >= 0) & (row < flat.rows) & (col >= 0) & (col < flat.cols)).astype(F32)
    w = flat.cols
    from_col = lax.broadcasted_iota(jnp.int32, (2 * w, 2 * w), 0)
    to_col = lax.broadcasted_iota(jnp.int32, (2 * w, 2 * w), 1)
    sorted_from = jnp.where(to_col < w, 2 * to_col, 2 * (to_col - w) + 1)
    order = (from_col == sorted_from).astype(F32)
    own[1:] = jnp.zeros((REPLAYS,) + own.shape[1:], BF16)
    packed[1:] = jnp.zeros((REPLAYS,) + packed.shape[1:], BF16)
    ext[...] = jnp.zeros(ext.shape, F32)
    perturb[...] = jnp.zeros(perturb.shape, F32)
    hidden[...] = jnp.zeros(hidden.shape, F32)
    for r in range(flat.rows):
        spot = flat.at(r, 0)
        ext[:, spot : spot + w] = target_in[r].astype(F32)
        for py in range(2):
            parts = dot(image_in[2 * r + py], order.astype(BF16))
            hidden[2 * py, :, spot : spot + w] = parts[:, :w]
            hidden[2 * py + 1, :, spot : spot + w] = parts[:, w:]
            parts = jnp.dot(
                perturb_in[2 * r + py],
                order,
                precision=lax.Precision.HIGHEST,
                preferred_element_type=F32,
            )
            perturb[2 * py, :, spot : spot + w] = parts[:, :w]
            perturb[2 * py + 1, :, spot : spot + w] = parts[:, w:]
    target_own[0] = ext[...].astype(BF16)
    packed[0, 4 * C : 5 * C, :] = dot(target_own[0], pack[...]).astype(BF16)
    for p in range(4):
        image[p] = hidden[p].astype(BF16)
        own[0, p] = (hidden[p] + perturb[p]).astype(BF16)
        packed[0, p * C : (p + 1) * C, :] = dot(own[0, p], pack[...]).astype(BF16)
    pl.semaphore_wait(barrier, greeted)

    def copy_of(source, target, sends, recvs, device):
        return pltpu.make_async_remote_copy(
            src_ref=source,
            dst_ref=target,
            send_sem=sends,
            recv_sem=recvs,
            device_id=device,
            device_id_type=MESH,
        )

    def rim_copies(from_own, from_packed, to_above, to_below, to_beside, k):
        copies = []

        def add(source, target, down, right):
            i = len(copies)
            device = {"rows": me_row + down, "cols": me_col + right}
            copy = copy_of(source, target, rim_sends.at[k, i], rim_recvs.at[k, i], device)
            copies.append((copy, exists(down, right), exists(-down, -right)))

        one, two = flat.lift, flat.lift + flat.edge
        add(from_own.at[:, :, one:two], to_above, 1, 0)
        one, two = flat.down_from, flat.down_from + flat.band
        add(from_own.at[:, :, one:two], to_below, -1, 0)
        if from_packed is not None:
            for j, (down, right) in enumerate(STEPS):
                add(from_packed, to_beside.at[j], -down, -right)
        return copies

    def start(copies):
        for copy, there, _ in copies:
            pl.when(there)(copy.start)

    def finish(copies):
        for copy, there, here in copies:
            pl.when(there)(copy.wait_send)
            pl.when(here)(copy.wait_recv)

    def rim_of(k):
        return rim_copies(own.at[k], packed.at[k], above.at[k], below.at[k], beside.at[k], k)

    begin = rim_of(0)
    start(begin)
    extra = rim_copies(target_own, None, target_above, target_below, None, REPLAYS + 1)
    start(extra)

    far_row, far_col = row + me_row * flat.rows, col + me_col * flat.cols
    inside = (
        (far_row >= 0)
        & (far_row < flat.rows * row_count)
        & (far_col >= 0)
        & (far_col < flat.cols * col_count)
    ).astype(F32)
    new_state[...] = state[...]
    new_moment[...] = moment[...]
    wide[...] = jnp.zeros(wide.shape, BF16)
    grad[...] = jnp.zeros(grad.shape, F32)
    lane = lax.broadcasted_iota(jnp.int32, (1, LANES), 1)
    has_above, has_below = me_row > 0, me_row < row_count - 1
    end = flat.down_from + flat.lift
    eye = (
        lax.broadcasted_iota(jnp.int32, (LANES, LANES), 0)
        == lax.broadcasted_iota(jnp.int32, (LANES, LANES), 1)
    ).astype(F32).astype(BF16)

    def chosen(packs, height):
        gathered = jnp.zeros((height, LANES), F32)
        for j, ((down, right), from_lane, pairs) in enumerate(flat.places()):
            keep = (lane >= from_lane) & (lane < from_lane + len(pairs)) & exists(down, right)
            gathered = gathered + jnp.where(keep, packs(j).astype(F32), 0.0)
        return gathered.astype(BF16)

    def extend(block, gathered, top, bottom):
        ext[...] = block.astype(F32) + dot(gathered, unpack[...])
        ext[:, 0 : flat.edge] += jnp.where(has_above, top.astype(F32), 0.0)
        ext[:, end:N] += jnp.where(has_below, bottom.astype(F32), 0.0)

    finish(begin)
    finish(extra)
    gathered = chosen(lambda j: beside[0, j, 4 * C : 5 * C], C)
    extend(target_own[0], gathered, target_above[0], target_below[0])
    target[...] = ext[...]

    def sum_copies(k):
        rows_out = []
        for d in range(1, row_count):
            there = position("rows", d)
            rows_out.append(
                copy_of(
                    sent.at[k, pl.ds(there * tall, tall)],
                    part_rows.at[k, d - 1],
                    sum_sends.at[k, d - 1],
                    sum_recvs.at[k, d - 1],
                    {"rows": there, "cols": me_col},
                )
            )
        cols_out = []
        for i, level in enumerate(levels):
            at = row_count - 1 + i
            cols_out.append(
                copy_of(
                    half.at[k, i],
                    part_cols.at[k, i],
                    sum_sends.at[k, at],
                    sum_recvs.at[k, at],
                    {"rows": me_row, "cols": partner(level)},
                )
            )
        band = pl.ds(me_row * tall, tall)
        back_out = []
        for d in range(1, row_count):
            at = row_count - 2 + len(levels) + d
            back_out.append(
                copy_of(
                    summed.at[k, band],
                    summed.at[k, band],
                    sum_sends.at[k, at],
                    sum_recvs.at[k, at],
                    {"rows": position("rows", d), "cols": me_col},
                )
            )
        return rows_out, cols_out, back_out

    def replay(k):
        fast = new_state[...].astype(BF16)
        ahead = dot_nt(eye, fast).astype(BF16)
        ahead_one, ahead_two = ahead[0:C, :], ahead[SECOND : SECOND + C, :]
        from_lane = lax.broadcasted_iota(jnp.int32, (LANES, K), 0)
        to_lane = lax.broadcasted_iota(jnp.int32, (LANES, K), 1)
        back_one = jnp.zeros((C, K), F32)
        for i in range(9):
            put = ((to_lane == from_lane + i * C) & (from_lane < C)).astype(F32).astype(BF16)
            back_one = back_one + dot(fast[i * C : (i + 1) * C, :], put)
        back_one = back_one.astype(BF16)
        four = 4 * C
        from_lane = lax.broadcasted_iota(jnp.int32, (LANES, four), 0)
        to_lane = lax.broadcasted_iota(jnp.int32, (LANES, four), 1)
        for py in range(2):
            for px in range(2):
                block = jnp.zeros((C, four), F32)
                for a, dy in ([(1, 0)] if py == 0 else [(0, 1), (2, 0)]):
                    for b, dx in ([(1, 0)] if px == 0 else [(0, 1), (2, 0)]):
                        i = 3 * a + b
                        slot = 2 * dy + dx
                        put = (
                            (to_lane == from_lane - SECOND + slot * C)
                            & (from_lane >= SECOND)
                            & (from_lane < SECOND + C)
                        ).astype(F32).astype(BF16)
                        block = block + dot(fast[i * C : (i + 1) * C, :], put)
                spread_weight[(2 * py + px) * C : (2 * py + px + 1) * C, :] = block.astype(BF16)

        gathered = chosen(lambda j: beside[k, j, 0 : 4 * C], 4 * C)
        for p in range(4):
            extend(own[k, p], gathered[p * C : (p + 1) * C, :], above[k, p], below[k, p])
            full = ext[...].astype(BF16)
            for i, (a, b) in enumerate(taps):
                moved = rolled(full, (a - 1) * T + (b - 1))
                attacked_cols[p, i * C : (i + 1) * C, :] = moved.astype(BF16)
            pre_value = dot(ahead_one, attacked_cols[p])
            sigmoid_value = jax.nn.sigmoid(pre_value)
            hidden[p] = pre_value * sigmoid_value * inside
            slope[p] = sigmoid_value * (1.0 + pre_value * (1.0 - sigmoid_value)) * inside
        for i, (a, b) in enumerate(taps):
            py, dy = [(1, -1), (0, 0), (1, 0)][a]
            px, dx = [(1, -1), (0, 0), (1, 0)][b]
            moved = rolled(hidden[2 * py + px].astype(BF16), dy * T + dx)
            hidden_cols[i * C : (i + 1) * C, :] = moved
        predict = dot(ahead_two, hidden_cols[...])
        ext[...] = predict
        residual = ((predict - target[...]) * inside).astype(BF16)
        wide[0:C, :] = jnp.zeros((C, high - low), BF16)
        wide[SECOND : SECOND + C, :] = (residual[:, low:high].astype(F32) * owned[:, low:high]).astype(BF16)
        total = dot_nt(hidden_cols[:, low:high], wide[...])
        wide[SECOND : SECOND + C, :] = jnp.zeros((C, high - low), BF16)
        for i, shift in enumerate((0, 1, T, T + 1)):
            rest_cols[i * C : (i + 1) * C, :] = rolled(residual, shift)
        hidden_grad = dot(spread_weight[...], rest_cols[...])
        for p in range(4):
            pre_grad = hidden_grad[p * C : (p + 1) * C, :] * slope[p]
            hidden[p] = pre_grad
            wide[0:C, :] = (pre_grad * owned)[:, low:high].astype(BF16)
            total = total + dot_nt(attacked_cols[p, :, low:high], wide[...])
        grad[0:K, :] = total
        sent[k] = grad[...].astype(BF16)
        rows_out, cols_out, back_out = sum_copies(k)
        for copy in rows_out:
            copy.start()

        def input_side(p):
            pre_grad = hidden[p].astype(BF16)
            for i, (a, b) in enumerate(taps):
                moved = rolled(pre_grad, -((a - 1) * T + (b - 1)))
                pre_cols[i * C : (i + 1) * C, :] = moved[:, low:high]
            input_grad = dot(back_one, pre_cols[...])
            moved = jnp.clip(
                perturb[p, :, low:high] + step_size * jnp.tanh(input_grad), -clip_bound, clip_bound
            )
            moved = moved * owned[:, low:high]
            perturb[p, :, low:high] = moved
            attacked = (image[p, :, low:high].astype(F32) + moved).astype(BF16)
            own[k + 1, p, :, low:high] = attacked
            packed[k + 1, p * C : (p + 1) * C, :] = dot(attacked, pack[low:high, :]).astype(BF16)

        input_side(0)
        for copy in rows_out:
            copy.wait()
        part = grad[pl.ds(pl.multiple_of(me_row * tall, 8), tall)]
        for d in range(1, row_count):
            part = part + part_rows[k, d - 1].astype(F32)
        for i in range(len(levels)):
            half[k, i] = part.astype(BF16)
            cols_out[i].start()
            if i < 2:
                input_side(i + 1)
            if i == 1:
                input_side(3)
                following = rim_of(k + 1)
                start(following)
            cols_out[i].wait()
            part = half[k, i].astype(F32) + part_cols[k, i].astype(F32)
        summed[k, pl.ds(pl.multiple_of(me_row * tall, 16), tall)] = part.astype(BF16)
        for copy in back_out:
            copy.start()
        for copy in back_out:
            copy.wait()
        now, later = updated(
            new_state[...], new_moment[...], summed[k, 0:K, :].astype(F32), K * C
        )
        new_state[...] = now
        new_moment[...] = later
        finish(following)

    @pl.loop(0, REPLAYS)
    def _(k):
        replay(k)

    for r in range(flat.rows):
        spot = flat.at(r, 0)
        predict_out[r] = ext[:, spot : spot + w].astype(BF16)
        for py in range(2):
            parts = jnp.concatenate(
                [perturb[2 * py, :, spot : spot + w], perturb[2 * py + 1, :, spot : spot + w]], axis=1
            )
            perturb_out[2 * r + py] = lax.dot_general(
                parts,
                order,
                (((1,), (1,)), ((), ())),
                precision=lax.Precision.HIGHEST,
                preferred_element_type=F32,
            )


def whole(flat, tables, image, perturb, target, state, moment, tall):
    C, N = flat.channels, flat.total
    K = 9 * C
    row_count, col_count = lax.axis_size("rows"), lax.axis_size("cols")
    levels = col_count.bit_length() - 1
    width = flat.own_high - flat.own_low
    short = tall // row_count
    operands = [image, perturb, target, state, moment, *tables]
    shapes = [
        jax.ShapeDtypeStruct(perturb.shape, F32),
        jax.ShapeDtypeStruct(target.shape, BF16),
        jax.ShapeDtypeStruct((K, LANES), F32),
        jax.ShapeDtypeStruct((K, LANES), F32),
    ]
    slots = REPLAYS + 1
    sums = 2 * (row_count - 1) + levels
    scratch = [
        pltpu.VMEM((C, N), F32),
        pltpu.VMEM((4, K, N), BF16),
        pltpu.VMEM((4, C, N), F32),
        pltpu.VMEM((4, C, N), F32),
        pltpu.VMEM((K, N), BF16),
        pltpu.VMEM((4 * C, N), BF16),
        pltpu.VMEM((K, width), BF16),
        pltpu.VMEM((LANES, width), BF16),
        pltpu.VMEM((4 * C, 4 * C), BF16),
        pltpu.VMEM((slots, 4, C, N), BF16),
        pltpu.VMEM((slots, 5 * C, LANES), BF16),
        pltpu.VMEM((C, N), F32),
        pltpu.VMEM((slots, 4, C, flat.edge), BF16),
        pltpu.VMEM((slots, 4, C, flat.band), BF16),
        pltpu.VMEM((slots, len(STEPS), 5 * C, LANES), BF16),
        pltpu.VMEM((1, C, flat.edge), BF16),
        pltpu.VMEM((1, C, flat.band), BF16),
        pltpu.VMEM((tall, LANES), F32),
        pltpu.VMEM((REPLAYS, tall, LANES), BF16),
        pltpu.VMEM((REPLAYS, row_count - 1, short, LANES), BF16),
        pltpu.VMEM((REPLAYS, levels, short, LANES), BF16),
        pltpu.VMEM((REPLAYS, levels, short, LANES), BF16),
        pltpu.VMEM((REPLAYS, tall, LANES), BF16),
        pltpu.SemaphoreType.DMA((slots + 1, 8)),
        pltpu.SemaphoreType.DMA((slots + 1, 8)),
        pltpu.SemaphoreType.DMA((REPLAYS, sums)),
        pltpu.SemaphoreType.DMA((REPLAYS, sums)),
        pltpu.VMEM((4, C, N), BF16),
        pltpu.VMEM((4, C, N), F32),
        pltpu.VMEM((1, C, N), BF16),
    ]
    return pl.pallas_call(
        functools.partial(whole_kernel, flat, row_count, col_count),
        out_shape=shapes,
        in_specs=[WHOLE] * len(operands),
        out_specs=[WHOLE] * len(shapes),
        scratch_shapes=scratch,
        compiler_params=pltpu.CompilerParams(
            collective_id=0, has_side_effects=True, vmem_limit_bytes=VMEM_LIMIT
        ),
    )(*operands)


def stacked(one, two):
    C = one.shape[0]
    one, two = (k.transpose(2, 3, 1, 0).reshape(9 * C, C) for k in (one, two))
    one = jnp.pad(one, ((0, 0), (0, SECOND - C)))
    two = jnp.pad(two, ((0, 0), (0, SECOND - C)))
    return jnp.concatenate([one, two], axis=1)


def unstacked(both, C):
    return tuple(
        both[:, low : low + C].reshape(3, 3, C, C).transpose(3, 2, 0, 1) for low in (0, SECOND)
    )


def body(image, perturb, target, kernel_one, kernel_two, moment_one, moment_two):
    C = image.shape[0]
    flat = Flat(C, target.shape[1], target.shape[2])
    tables = tuple(jnp.asarray(t) for t in flat.tables())
    pieces = 16 * lax.axis_size("rows")
    tall = -(-9 * C // pieces) * pieces
    state = stacked(kernel_one, kernel_two)
    moment = stacked(moment_one, moment_two)
    image, perturb, target = (x.transpose(1, 0, 2) for x in (image, perturb, target))
    perturb, predict, state, moment = whole(
        flat, tables, image, perturb, target, state, moment, tall
    )
    new_one, new_two = unstacked(state, C)
    new_moment_one, new_moment_two = unstacked(moment, C)
    perturb, prediction = perturb.transpose(1, 0, 2), predict.transpose(1, 0, 2)
    return (perturb, prediction, new_one, new_two, new_moment_one, new_moment_two)


def solution(mesh):
    in_specs = (
        P(None, "rows", "cols"),
        P(None, "rows", "cols"),
        P(None, "rows", "cols"),
        P(),
        P(),
        P(),
        P(),
    )
    out_specs = (P(None, "rows", "cols"), P(None, "rows", "cols"), P(), P(), P(), P())
    return jax.shard_map(body, mesh=mesh, in_specs=in_specs, out_specs=out_specs, check_vma=False)
```
